256 devices in a mesh: grp: 4 (over x), own: 64 (over y, z, core).
Axes of the slice: x: 4, y: 4, z: 8, core: 2. Of those that a mesh axis runs over, the one named last changes fastest.
Arguments:
- grad_parts: float32 [4, 64, 4, 64, 16, 2, 128], P('grp', 'own'), may hold values from -6 to 6
- block_ids: int32 [64, 4, 64, 16], P('own'), may hold values from 0 to 1023, as said below
- block_counts: int32 [64, 4, 64], P('own'), may hold values from 0 to 16, as said below
- params: float32 [8, 32768, 2, 128], P(None, ('grp', 'own')), may hold values from -4 to 4
- first_moment: float32 [8, 32768, 2, 128], P(None, ('grp', 'own')), may hold values from -2 to 2
- second_moment: float32 [8, 32768, 2, 128], P(None, ('grp', 'own')), may hold values from 0.0001 to 0.03
Outputs:
- new_params: float32 [8, 32768, 2, 128], P(None, ('grp', 'own'))
- new_first: float32 [8, 32768, 2, 128], P(None, ('grp', 'own'))
- new_second: float32 [8, 32768, 2, 128], P(None, ('grp', 'own'))
The draws below stay inside these ranges and needn't reach their ends.
Inputs may be any that keep to these rules, and one draw needn't show every extreme that they name: `block_ids`: within one row (fixed group and destination) the 16 block numbers are distinct; numbers in slots beyond the count are arbitrary but in range. `block_counts`: some destination device gets 16 used slots from every ray group.
All inputs are finite; a program needn't handle non-finite values.
Results may differ from the reference program's by a relative error of at most 0.00002.
Values sent between devices are 32-bit elements; how exact they have to be, the bound alone decides.
No kernel may reach another device: no remote copies, remote signals or barrier semaphores. Data moves between devices by JAX's collectives and lax.ppermute only.
A program may use at most 64 MiB of HBM per device.

```python
import math
import jax
import jax.numpy as jnp
from jax import lax

LEVELS = 8
ENTRIES = 4194304
FEATURES = 2
BLOCK = 128
SLOTS = 16
NBLK = 32768
N_GRP = 4
N_OWN = 64
DEVICES = 256


def device_ramp(top):
    position = jnp.arange(N_GRP, dtype=jnp.float32)[:, None] * N_OWN + jnp.arange(N_OWN, dtype=jnp.float32)[None, :]
    level = jnp.exp(jnp.log(top) * position / (N_GRP * N_OWN - 1))
    return level.reshape(1, 1, N_GRP, N_OWN, 1, 1, 1)


def draw_grad_parts(key, part):
    shape = (N_GRP, N_OWN, N_GRP, N_OWN, SLOTS, FEATURES, BLOCK)
    ramp = device_ramp(8.0)
    values = 0.5 * ramp * jax.random.normal(jax.random.fold_in(key, 41), shape, dtype=jnp.float32)
    return jnp.clip(values, -6.0, 6.0).astype(jnp.float32)


def draw_block_ids(key, part):
    total = LEVELS * (ENTRIES // BLOCK // DEVICES)
    count_rows = N_OWN * N_GRP * N_OWN
    limit = 2 ** 31 // total - 1
    scores = jax.random.randint(jax.random.fold_in(key, 11), (count_rows, total), 0, limit, dtype=jnp.int32)
    scores = scores * total + jnp.arange(total, dtype=jnp.int32)[None, :]
    values, picked = lax.top_k(scores, SLOTS)
    return picked.astype(jnp.int32).reshape(N_OWN, N_GRP, N_OWN, SLOTS)


def draw_block_counts(key, part):
    first, second, third = jax.random.split(jax.random.fold_in(key, 23), 3)
    counts = jax.random.randint(first, (N_OWN, N_GRP, N_OWN), 0, SLOTS + 1, dtype=jnp.int32)
    row_grp = jax.random.randint(second, (), 0, N_GRP, dtype=jnp.int32)
    row_own = jax.random.randint(third, (), 0, N_OWN, dtype=jnp.int32)
    return counts.at[:, row_grp, row_own].set(SLOTS)


def levels(own_key, shape, shards, smallest, high):
    level = 1.0
    for dim, blocks in shards:
        draws = jax.random.uniform(jax.random.fold_in(jax.random.fold_in(own_key, 6), dim), (blocks,), jnp.float32, smallest / len(shards), high / len(shards))
        level = level * jnp.repeat(jnp.exp(draws), shape[dim] // blocks).reshape((-1,) + (1,) * (len(shape) - 1 - dim))
    return level


def gaussian(own_key, extent, scale, most, shards=(), kind=jnp.bfloat16):
    factor_of = levels(own_key, extent, shards, -0.22, 0.18) if shards else 1.0
    array = jax.random.normal(own_key, extent, jnp.float32) * scale * factor_of
    return jnp.minimum(jnp.maximum(array, -most), most).astype(kind)


def setup_inputs(seed: int = 0) -> dict:
    keys = jax.random.split(jax.random.key(seed), 7)
    return {
        "grad_parts": draw_grad_parts(jax.random.fold_in(keys[6], 71), 0),
        "block_ids": draw_block_ids(jax.random.fold_in(keys[6], 71), 0),
        "block_counts": draw_block_counts(jax.random.fold_in(keys[6], 71), 0),
        "params": gaussian(keys[3], (LEVELS, NBLK, FEATURES, BLOCK), 0.5, 4.0, ((1, 256),), jnp.float32),
        "first_moment": gaussian(keys[4], (LEVELS, NBLK, FEATURES, BLOCK), 0.3, 2.0, ((1, 256),), jnp.float32),
        "second_moment": jnp.clip(jnp.exp(math.log(0.03) - 5.7037825 * jax.random.uniform(keys[5], (LEVELS, NBLK, FEATURES, BLOCK), jnp.float32) ** levels(keys[5], (LEVELS, NBLK, FEATURES, BLOCK), ((1, 256),), -0.2, 0.2)), 0.0001, 0.03),
    }


def reference(grad_parts, block_ids, block_counts, params, first_moment, second_moment):
    blocks_level = ENTRIES // BLOCK
    per_device = blocks_level // DEVICES
    summed = lax.optimization_barrier(jnp.sum(grad_parts, axis=0))
    dest = jnp.arange(N_GRP, dtype=jnp.int32)[:, None] * N_OWN + jnp.arange(N_OWN, dtype=jnp.int32)[None, :]
    level = block_ids // per_device
    within = block_ids % per_device
    target = (level * blocks_level + dest[None, :, :, None] * per_device + within).astype(jnp.int32)
    valid = jnp.arange(SLOTS, dtype=jnp.int32)[None, None, None, :] < block_counts[..., None]
    width = FEATURES * BLOCK
    rows = summed.reshape(-1, width) * valid.reshape(-1, 1).astype(jnp.float32)
    segments = LEVELS * blocks_level
    dense = jax.ops.segment_sum(rows, target.reshape(-1), num_segments=segments)
    hits = jax.ops.segment_sum(valid.reshape(-1).astype(jnp.int32), target.reshape(-1), num_segments=segments) > 0
    square = jnp.sum(dense * dense)
    count = jnp.sum(hits.astype(jnp.float32))
    rms = jnp.sqrt(square / (count * width) + 1e-06)
    scale = jnp.minimum(jnp.float32(1.0), 0.5 / rms)
    clipped = scale * dense
    old_p = params.reshape(segments, width)
    old_m = first_moment.reshape(segments, width)
    old_v = second_moment.reshape(segments, width)
    mask = hits[:, None]
    new_m = jnp.where(mask, 0.9 * old_m + 0.1 * clipped, old_m)
    new_v = jnp.where(mask, 0.99 * old_v + 0.01 * clipped * clipped, old_v)
    stepped = old_p - 0.01 * (new_m / (1.0 - 0.9 ** 8)) / (jnp.sqrt(new_v / (1.0 - 0.99 ** 8)) + 1e-08)
    new_p = jnp.where(mask, stepped, old_p)
    shape = params.shape
    return (new_p.reshape(shape), new_m.reshape(shape), new_v.reshape(shape))
```

```python
import functools

import jax
import jax.numpy as jnp
from jax import lax
from jax.experimental import pallas as pl
from jax.experimental.pallas import tpu as pltpu
from jax.sharding import Mesh
from jax.sharding import PartitionSpec as P


OWN = ("own_0", "own_1", "own_2")
GRP_OWN = ("grp", "own_0", "own_1", "own_2")
CHUNKS = (8, 8)
STEPS = 4
f32 = jnp.float32
ANY = pl.BlockSpec(memory_space=pl.ANY)
VMEM = pl.BlockSpec(memory_space=pltpu.VMEM)
SMEM = pl.BlockSpec(memory_space=pltpu.SMEM)


def kernel_call(body, outs, ins, out_specs, scratch=(), aliases=None, moved=1 << 20):
    return pl.pallas_call(
        body,
        out_shape=outs,
        in_specs=ins,
        out_specs=out_specs,
        scratch_shapes=list(scratch),
        input_output_aliases=aliases or {},
        compiler_params=pltpu.CompilerParams(vmem_limit_bytes=16 << 20),
        cost_estimate=pl.CostEstimate(flops=1 << 18, bytes_accessed=moved, transcendentals=0),
    )


def copies_kernel(plan, order, partial, *rest):
    outs, sems = rest[:-1], rest[-1]
    started = []
    for number, (output, entry, which, part, rows) in enumerate(plan):
        half = partial.shape[1] // 2
        source = partial.at[
            order[which], pl.ds(part * half, half), pl.ds(rows[0], rows[1] - rows[0])
        ]
        target = outs[output] if entry is None else outs[output].at[entry]
        copy = pltpu.make_async_copy(source, target, sems.at[number])
        copy.start()
        started.append(copy)
    for copy in started:
        copy.wait()


def add_kernel(top_own, low_own, top_in, low_in, top_out, low_out):
    top_out[...] = top_own[...] + top_in[1]
    low_out[...] = low_own[...] + low_in[1]


def join_kernel(
    top_own, low_own, top_near, low_near, top_far, low_far, before, out
):
    half, _ = top_far.shape[:2]
    done = before.shape[1]
    out[:, 0:done] = before[...]
    out[0:half, done:] = top_own[...] + top_near[0] + top_far[...]
    out[half:, done:] = low_own[...] + low_near[0] + low_far[...]


def sum_kernel(top_own, low_own, top_near, low_near, top_far, low_far, out):
    half = top_far.shape[0]
    out[0:half] = top_own[...] + top_near[0] + top_far[...]
    out[half:] = low_own[...] + low_near[0] + low_far[...]


def pair_rows(t):
    return pl.ds(pl.multiple_of(t * 2, 2), 2)


def mark_kernel(slots, target, mask, count):
    mask[...] = jnp.zeros_like(mask)
    ones = jnp.ones((2, mask.shape[1]), f32)

    def source(s, carry):
        for j in range(slots):
            mask[pair_rows(target[s * slots + j])] = ones
        return carry

    lax.fori_loop(0, target.shape[0] // slots, source, 0)
    count[...] = jnp.sum(mask[0 : mask.shape[0] - 8], axis=0, keepdims=True)


def scatter_kernel(slots, target, rows, count, dense, message):
    dense[...] = jnp.zeros_like(dense)

    def source(s, carry):
        base = s * slots
        at = [target[base + j] for j in range(slots)]
        new = [dense[pair_rows(t)] + rows[pair_rows(base + j)] for j, t in enumerate(at)]
        for t, v in zip(at, new):
            dense[pair_rows(t)] = v
        return carry

    lax.fori_loop(0, target.shape[0] // slots, source, 0)
    values = dense[0 : dense.shape[0] - 8]
    square = jnp.sum(jnp.sum(values * values, axis=0, keepdims=True), axis=1, keepdims=True)
    touched = jnp.sum(count[...], axis=1, keepdims=True)
    lane = lax.broadcasted_iota(jnp.int32, (1, 128), 1)
    row = jnp.where(lane == 0, square, jnp.where(lane == 1, touched, 0.0))
    message[...] = jnp.broadcast_to(row, message.shape)


def update_kernel(messages, dense, mask, p_in, m_in, v_in, *rest):
    outs, held, made, sems, done = rest[:3], rest[3:6], rest[6:9], rest[9], rest[10]
    size = p_in.shape[0] // STEPS
    spans = [pl.ds(step * size, size) for step in range(STEPS)]
    loads = []
    for step, at in enumerate(spans):
        for k, source in enumerate((p_in, m_in, v_in)):
            copy = pltpu.make_async_copy(source.at[at], held[k].at[at], sems.at[k, step])
            copy.start()
            loads.append(copy)
    total = jnp.sum(messages[...], axis=0, keepdims=True)
    square, touched = total[0:1, 0:1], total[0:1, 1:2]
    rms = jnp.sqrt(square / touched + 1e-06)
    scale = jnp.minimum(jnp.float32(1.0), 0.5 / rms)
    first, second = 0.1 * scale, 0.01 * scale * scale
    copies = []
    for step, at in enumerate(spans):
        for copy in loads[3 * step : 3 * step + 3]:
            copy.wait()
        grad, live = dense[at], mask[at]
        new_m = held[1][at] * (1.0 - 0.1 * live) + first * grad
        new_v = held[2][at] * (1.0 - 0.01 * live) + second * grad * grad
        root = jnp.sqrt(new_v * (1.0 / (1.0 - 0.99**8))) + 1e-08
        made[0][at] = held[0][at] - (live * (0.01 / (1.0 - 0.9**8))) * new_m / root
        made[1][at] = new_m
        made[2][at] = new_v
        for k in range(3):
            copy = pltpu.make_async_copy(made[k].at[at], outs[k].at[at], done.at[k, step])
            copy.start()
            copies.append(copy)
    for copy in copies:
        copy.wait()


def in_hbm(array):
    return pltpu.with_memory_space_constraint(array, pltpu.HBM)


def shape(*dims):
    return jax.ShapeDtypeStruct(dims, f32)


def step(grad_parts, block_ids, block_counts, params, first_moment, second_moment):
    member = lax.axis_index("grp")
    _, _, groups, owners, slots, features, lanes = grad_parts.shape
    blocks = params.shape[0] * params.shape[1]
    devices = groups * owners
    half = owners // 2
    partial = in_hbm(grad_parts.reshape(groups, owners, slots * features, lanes))

    ids = lax.dynamic_index_in_dim(block_ids[0], member, 0, keepdims=False)
    counts = lax.dynamic_index_in_dim(block_counts[0], member, 0, keepdims=False)
    valid = jnp.arange(slots, dtype=jnp.int32)[None, :] < counts[:, None]
    named = jnp.where(valid, ids, blocks).astype(f32)
    named = jnp.pad(named, ((0, 0), (0, lanes - slots))).reshape(owners, 1, lanes)
    named = lax.all_to_all(named, OWN, split_axis=0, concat_axis=0, tiled=True)
    target = named.reshape(owners, lanes)[:, :slots].astype(jnp.int32).reshape(-1)

    flip, mirror = member ^ 1, 3 - member
    order = jnp.stack([flip, mirror, mirror ^ 1, member])
    flips = [(k, k ^ 1) for k in range(groups)]
    mirrors = [(k, 3 - k) for k in range(groups)]

    def copied(outs, plan):
        return kernel_call(
            functools.partial(copies_kernel, plan),
            outs,
            [SMEM, ANY],
            (VMEM,) * len(outs),
            [pltpu.SemaphoreType.DMA((len(plan),))],
            moved=2 * len(plan) << 18,
        )(order, partial)

    spans = [(sum(CHUNKS[:k]) * features, sum(CHUNKS[: k + 1]) * features) for k in (0, 1)]
    arrived = []
    for span in spans:
        size = span[1] - span[0]
        both = shape(2, half, size, lanes)
        plan = ((0, 0, 0, 0, span), (1, 0, 1, 1, span), (0, 1, 2, 0, span), (1, 1, 2, 1, span))
        top, low = copied((both, both), plan)
        top_in = lax.ppermute(top, "grp", flips)
        low_in = lax.ppermute(low, "grp", mirrors)
        arrived.append([top_in, low_in])
    outs, plan = [], []
    for span in spans:
        for which, part in ((1, 0), (0, 1), (3, 0), (3, 1)):
            plan.append((len(outs), None, which, part, span))
            outs.append(shape(half, span[1] - span[0], lanes))
    kept = copied(tuple(outs), tuple(plan))
    share = None
    for k, span in enumerate(spans):
        size = span[1] - span[0]
        piece = shape(half, size, lanes)
        top_in, low_in = arrived[k]
        far_top, far_low, own_top, own_low = kept[4 * k : 4 * k + 4]
        top, low = kernel_call(add_kernel, (piece, piece), [VMEM] * 4, (VMEM, VMEM))(
            far_top, far_low, top_in, low_in
        )
        top_far = lax.ppermute(top, "grp", mirrors)
        low_far = lax.ppermute(low, "grp", flips)
        pieces = (own_top, own_low, top_in, low_in, top_far, low_far)
        if share is None:
            share = kernel_call(sum_kernel, shape(owners, size, lanes), [VMEM] * 6, VMEM)(*pieces)
        else:
            share = kernel_call(
                join_kernel, shape(owners, span[1], lanes), [VMEM] * 7, VMEM
            )(*pieces, share)
    share = lax.all_to_all(share, OWN, split_axis=0, concat_axis=0, tiled=True)
    share = share.reshape(owners * slots * features, lanes)

    rows = blocks * features
    table = shape(rows + 8, lanes)
    mask, count = kernel_call(
        functools.partial(mark_kernel, slots), (table, shape(1, lanes)), [SMEM], (VMEM, VMEM)
    )(target)
    dense, message = kernel_call(
        functools.partial(scatter_kernel, slots),
        (table, shape(devices, lanes)),
        [SMEM, VMEM, VMEM],
        (VMEM, VMEM),
    )(target, share, count)
    messages = lax.all_to_all(
        message.reshape(devices, 1, lanes), GRP_OWN, split_axis=0, concat_axis=0, tiled=True
    ).reshape(devices, lanes)
    flat = shape(rows, lanes)
    state = [in_hbm(a.reshape(rows, lanes)) for a in (params, first_moment, second_moment)]
    outs = kernel_call(
        update_kernel,
        (flat,) * 3,
        [VMEM] * 3 + [ANY] * 3,
        (ANY,) * 3,
        [pltpu.VMEM((rows, lanes), f32)] * 6 + [pltpu.SemaphoreType.DMA((3, STEPS))] * 2,
    )(messages, dense, mask, *state)
    return tuple(out.reshape(params.shape) for out in outs)


def solution(mesh):
    split = Mesh(
        mesh.devices.reshape(mesh.shape["grp"], 4, 8, 2), ("grp", "own_0", "own_1", "own_2")
    )
    in_specs = (
        P("grp", OWN, None, None, None, None, None),
        P(OWN, None, None, None),
        P(OWN, None, None),
        P(None, GRP_OWN, None, None),
        P(None, GRP_OWN, None, None),
        P(None, GRP_OWN, None, None),
    )
    out_specs = (
        P(None, GRP_OWN, None, None),
        P(None, GRP_OWN, None, None),
        P(None, GRP_OWN, None, None),
    )
    return jax.shard_map(step, mesh=split, in_specs=in_specs, out_specs=out_specs, check_vma=False)
```

```python
import functools

import jax
import jax.numpy as jnp
from jax import lax
from jax.experimental import pallas as pl
from jax.experimental.pallas import tpu as pltpu
from jax.sharding import Mesh
from jax.sharding import PartitionSpec as P


OWN = ("own_0", "own_1", "own_2")
GRP_OWN = ("grp", "own_0", "own_1", "own_2")
CHUNKS = (8, 8)
STEPS = 4
f32 = jnp.float32
ANY = pl.BlockSpec(memory_space=pl.ANY)
VMEM = pl.BlockSpec(memory_space=pltpu.VMEM)
SMEM = pl.BlockSpec(memory_space=pltpu.SMEM)


def kernel_call(body, outs, ins, out_specs, scratch=(), aliases=None, moved=1 << 20):
    return pl.pallas_call(
        body,
        out_shape=outs,
        in_specs=ins,
        out_specs=out_specs,
        scratch_shapes=list(scratch),
        input_output_aliases=aliases or {},
        compiler_params=pltpu.CompilerParams(vmem_limit_bytes=16 << 20),
        cost_estimate=pl.CostEstimate(flops=1 << 18, bytes_accessed=moved, transcendentals=0),
    )


def copies_kernel(plan, order, partial, *rest):
    outs, sems = rest[:-1], rest[-1]
    started = []
    for number, (output, entry, which, part, rows) in enumerate(plan):
        half = partial.shape[1] // 2
        source = partial.at[
            order[which], pl.ds(part * half, half), pl.ds(rows[0], rows[1] - rows[0])
        ]
        target = outs[output] if entry is None else outs[output].at[entry]
        copy = pltpu.make_async_copy(source, target, sems.at[number])
        copy.start()
        started.append(copy)
    for copy in started:
        copy.wait()


def add_kernel(top_own, low_own, top_in, low_in, top_out, low_out):
    top_out[...] = top_own[...] + top_in[1]
    low_out[...] = low_own[...] + low_in[1]


def sum_kernel(top_own, low_own, top_near, low_near, top_far, low_far, out):
    half = top_far.shape[0]
    out[0:half] = top_own[...] + top_near[0] + top_far[...]
    out[half:] = low_own[...] + low_near[0] + low_far[...]


def pair_rows(t):
    return pl.ds(pl.multiple_of(t * 2, 2), 2)


def mark_kernel(slots, target, mask, count):
    mask[...] = jnp.zeros_like(mask)
    ones = jnp.ones((2, mask.shape[1]), f32)

    def source(s, carry):
        for j in range(slots):
            mask[pair_rows(target[s * slots + j])] = ones
        return carry

    lax.fori_loop(0, target.shape[0] // slots, source, 0)
    count[...] = jnp.sum(mask[0 : mask.shape[0] - 8], axis=0, keepdims=True)


def scatter_rows(slots, first, width, target, rows, even, odd):
    even[...] = jnp.zeros_like(even)
    odd[...] = jnp.zeros_like(odd)

    def sources(s, carry):
        picks = []
        for k, ref in ((0, even), (1, odd)):
            for j in range(width):
                picks.append((ref, target[(2 * s + k) * slots + first + j]))
        new = [
            ref[pair_rows(t)] + rows[pair_rows(2 * s * width + j)]
            for j, (ref, t) in enumerate(picks)
        ]
        for (ref, t), value in zip(picks, new):
            ref[pair_rows(t)] = value
        return carry

    lax.fori_loop(0, target.shape[0] // (2 * slots), sources, 0)


def first_kernel(slots, width, target, rows, dense, other):
    scatter_rows(slots, 0, width, target, rows, dense, other)
    dense[...] += other[...]


def last_kernel(slots, first, width, target, rows, before, count, dense, message, other):
    scatter_rows(slots, first, width, target, rows, dense, other)
    dense[...] += other[...] + before[...]
    values = dense[0 : dense.shape[0] - 8]
    square = jnp.sum(jnp.sum(values * values, axis=0, keepdims=True), axis=1, keepdims=True)
    touched = jnp.sum(count[...], axis=1, keepdims=True)
    lane = lax.broadcasted_iota(jnp.int32, (1, 128), 1)
    row = jnp.where(lane == 0, square, jnp.where(lane == 1, touched, 0.0))
    message[...] = jnp.broadcast_to(row, message.shape)


def update_kernel(messages, dense, mask, p_in, m_in, v_in, *rest):
    outs, held, made, sems, done = rest[:3], rest[3:6], rest[6:9], rest[9], rest[10]
    size = p_in.shape[0] // STEPS
    spans = [pl.ds(step * size, size) for step in range(STEPS)]
    loads = []
    for step, at in enumerate(spans):
        for k, source in enumerate((p_in, m_in, v_in)):
            copy = pltpu.make_async_copy(source.at[at], held[k].at[at], sems.at[k, step])
            copy.start()
            loads.append(copy)
    total = jnp.sum(messages[...], axis=0, keepdims=True)
    square, touched = total[0:1, 0:1], total[0:1, 1:2]
    rms = jnp.sqrt(square / touched + 1e-06)
    scale = jnp.minimum(jnp.float32(1.0), 0.5 / rms)
    first, second = 0.1 * scale, 0.01 * scale * scale
    copies = []
    for step, at in enumerate(spans):
        for copy in loads[3 * step : 3 * step + 3]:
            copy.wait()
        grad, live = dense[at], mask[at]
        new_m = held[1][at] * (1.0 - 0.1 * live) + first * grad
        new_v = held[2][at] * (1.0 - 0.01 * live) + second * grad * grad
        root = jnp.sqrt(new_v * (1.0 / (1.0 - 0.99**8))) + 1e-08
        made[0][at] = held[0][at] - (live * (0.01 / (1.0 - 0.9**8))) * new_m / root
        made[1][at] = new_m
        made[2][at] = new_v
        for k in range(3):
            copy = pltpu.make_async_copy(made[k].at[at], outs[k].at[at], done.at[k, step])
            copy.start()
            copies.append(copy)
    for copy in copies:
        copy.wait()


def in_hbm(array):
    return pltpu.with_memory_space_constraint(array, pltpu.HBM)


def shape(*dims):
    return jax.ShapeDtypeStruct(dims, f32)


def step(grad_parts, block_ids, block_counts, params, first_moment, second_moment):
    member = lax.axis_index("grp")
    _, _, groups, owners, slots, features, lanes = grad_parts.shape
    blocks = params.shape[0] * params.shape[1]
    devices = groups * owners
    half = owners // 2
    partial = in_hbm(grad_parts.reshape(groups, owners, slots * features, lanes))

    ids = lax.dynamic_index_in_dim(block_ids[0], member, 0, keepdims=False)
    counts = lax.dynamic_index_in_dim(block_counts[0], member, 0, keepdims=False)
    valid = jnp.arange(slots, dtype=jnp.int32)[None, :] < counts[:, None]
    named = jnp.where(valid, ids, blocks).astype(f32)
    named = jnp.pad(named, ((0, 0), (0, lanes - slots))).reshape(owners, 1, lanes)
    named = lax.all_to_all(named, OWN, split_axis=0, concat_axis=0, tiled=True)
    target = named.reshape(owners, lanes)[:, :slots].astype(jnp.int32).reshape(-1)

    flip, mirror = member ^ 1, 3 - member
    order = jnp.stack([flip, mirror, mirror ^ 1, member])
    flips = [(k, k ^ 1) for k in range(groups)]
    mirrors = [(k, 3 - k) for k in range(groups)]

    def copied(outs, plan):
        return kernel_call(
            functools.partial(copies_kernel, plan),
            outs,
            [SMEM, ANY],
            (VMEM,) * len(outs),
            [pltpu.SemaphoreType.DMA((len(plan),))],
            moved=2 * len(plan) << 18,
        )(order, partial)

    spans = [(sum(CHUNKS[:k]) * features, sum(CHUNKS[: k + 1]) * features) for k in (0, 1)]
    shares = []
    for span in spans:
        size = span[1] - span[0]
        piece, both = shape(half, size, lanes), shape(2, half, size, lanes)
        plan = ((0, 0, 0, 0, span), (1, 0, 1, 1, span), (0, 1, 2, 0, span), (1, 1, 2, 1, span))
        top, low = copied((both, both), plan)
        top_in = lax.ppermute(top, "grp", flips)
        low_in = lax.ppermute(low, "grp", mirrors)
        plan = tuple(
            (n, None, which, part, span)
            for n, (which, part) in enumerate(((1, 0), (0, 1), (3, 0), (3, 1)))
        )
        far_top, far_low, own_top, own_low = copied((piece,) * 4, plan)
        top, low = kernel_call(add_kernel, (piece, piece), [VMEM] * 4, (VMEM, VMEM))(
            far_top, far_low, top_in, low_in
        )
        top_far = lax.ppermute(top, "grp", mirrors)
        low_far = lax.ppermute(low, "grp", flips)
        share = kernel_call(sum_kernel, shape(owners, size, lanes), [VMEM] * 6, VMEM)(
            own_top, own_low, top_in, low_in, top_far, low_far
        )
        share = lax.all_to_all(share, OWN, split_axis=0, concat_axis=0, tiled=True)
        shares.append(share.reshape(owners * size, lanes))

    rows = blocks * features
    table = shape(rows + 8, lanes)
    mask, count = kernel_call(
        functools.partial(mark_kernel, slots), (table, shape(1, lanes)), [SMEM], (VMEM, VMEM)
    )(target)
    spare = [pltpu.VMEM(table.shape, f32)]
    before = kernel_call(
        functools.partial(first_kernel, slots, CHUNKS[0]), table, [SMEM, VMEM], VMEM, spare
    )(target, shares[0])
    dense, message = kernel_call(
        functools.partial(last_kernel, slots, CHUNKS[0], CHUNKS[1]),
        (table, shape(devices, lanes)),
        [SMEM] + [VMEM] * 3,
        (VMEM, VMEM),
        spare,
    )(target, shares[1], before, count)
    messages = lax.all_to_all(
        message.reshape(devices, 1, lanes), GRP_OWN, split_axis=0, concat_axis=0, tiled=True
    ).reshape(devices, lanes)
    flat = shape(rows, lanes)
    state = [in_hbm(a.reshape(rows, lanes)) for a in (params, first_moment, second_moment)]
    outs = kernel_call(
        update_kernel,
        (flat,) * 3,
        [VMEM] * 3 + [ANY] * 3,
        (ANY,) * 3,
        [pltpu.VMEM((rows, lanes), f32)] * 6 + [pltpu.SemaphoreType.DMA((3, STEPS))] * 2,
    )(messages, dense, mask, *state)
    return tuple(out.reshape(params.shape) for out in outs)


def solution(mesh):
    split = Mesh(
        mesh.devices.reshape(mesh.shape["grp"], 4, 8, 2), ("grp", "own_0", "own_1", "own_2")
    )
    in_specs = (
        P("grp", OWN, None, None, None, None, None),
        P(OWN, None, None, None),
        P(OWN, None, None),
        P(None, GRP_OWN, None, None),
        P(None, GRP_OWN, None, None),
        P(None, GRP_OWN, None, None),
    )
    out_specs = (
        P(None, GRP_OWN, None, None),
        P(None, GRP_OWN, None, None),
        P(None, GRP_OWN, None, None),
    )
    return jax.shard_map(step, mesh=split, in_specs=in_specs, out_specs=out_specs, check_vma=False)
```

```python
import functools

import jax
import jax.numpy as jnp
from jax import lax
from jax.experimental import pallas as pl
from jax.experimental.pallas import tpu as pltpu
from jax.sharding import Mesh
from jax.sharding import PartitionSpec as P


OWN = ("own_0", "own_1", "own_2")
GRP_OWN = ("grp", "own_0", "own_1", "own_2")
CHUNKS = (4, 12)
STEPS = 4
f32 = jnp.float32
ANY = pl.BlockSpec(memory_space=pl.ANY)
VMEM = pl.BlockSpec(memory_space=pltpu.VMEM)
SMEM = pl.BlockSpec(memory_space=pltpu.SMEM)


def kernel_call(body, outs, ins, out_specs, scratch=(), aliases=None, moved=1 << 20):
    return pl.pallas_call(
        body,
        out_shape=outs,
        in_specs=ins,
        out_specs=out_specs,
        scratch_shapes=list(scratch),
        input_output_aliases=aliases or {},
        compiler_params=pltpu.CompilerParams(vmem_limit_bytes=16 << 20),
        cost_estimate=pl.CostEstimate(flops=1 << 18, bytes_accessed=moved, transcendentals=0),
    )


def copies_kernel(plan, order, partial, *rest):
    outs, sems = rest[:-1], rest[-1]
    started = []
    for number, (output, entry, which, part, rows) in enumerate(plan):
        half = partial.shape[1] // 2
        source = partial.at[
            order[which], pl.ds(part * half, half), pl.ds(rows[0], rows[1] - rows[0])
        ]
        target = outs[output] if entry is None else outs[output].at[entry]
        copy = pltpu.make_async_copy(source, target, sems.at[number])
        copy.start()
        started.append(copy)
    for copy in started:
        copy.wait()


def add_kernel(top_own, low_own, top_in, low_in, top_out, low_out):
    top_out[...] = top_own[...] + top_in[...]
    low_out[...] = low_own[...] + low_in[...]


def sum_kernel(top_own, low_own, top_near, low_near, top_far, low_far, out):
    half = top_far.shape[0]
    out[0:half] = top_own[...] + top_near[...] + top_far[...]
    out[half:] = low_own[...] + low_near[...] + low_far[...]


def first_add_kernel(top_own, low_own, top_in, low_in, top_out, low_out):
    top_out[...] = top_own[...] + top_in[1]
    low_out[...] = low_own[...] + low_in[1]


def first_sum_kernel(top_own, low_own, top_near, low_near, top_far, low_far, named, out):
    half, size = top_far.shape[:2]
    pitch = out.shape[0] // (2 * half)
    out[...] = jnp.zeros_like(out)
    for o in range(half):
        out[o * pitch : o * pitch + size] = top_own[o] + top_near[0, o] + top_far[o]
        at = (half + o) * pitch
        out[at : at + size] = low_own[o] + low_near[0, o] + low_far[o]
    for o in range(2 * half):
        at = o * pitch + size
        out[at : at + 1] = named[o : o + 1]


def pair_rows(t):
    return pl.ds(pl.multiple_of(t * 2, 2), 2)


def mark_kernel(slots, target, mask, count):
    mask[...] = jnp.zeros_like(mask)
    ones = jnp.ones((2, mask.shape[1]), f32)

    def source(s, carry):
        for j in range(slots):
            mask[pair_rows(target[s * slots + j])] = ones
        return carry

    lax.fori_loop(0, target.shape[0] // slots, source, 0)
    count[...] = jnp.sum(mask[0 : mask.shape[0] - 8], axis=0, keepdims=True)


def scatter_rows(slots, first, width, pitch, target, rows, even, odd):
    even[...] = jnp.zeros_like(even)
    odd[...] = jnp.zeros_like(odd)

    def sources(s, carry):
        picks = []
        for k, ref in ((0, even), (1, odd)):
            for j in range(width):
                t = target[(2 * s + k) * slots + first + j]
                picks.append((ref, t, (2 * s + k) * pitch + j))
        new = [ref[pair_rows(t)] + rows[pair_rows(at)] for ref, t, at in picks]
        for (ref, t, _), value in zip(picks, new):
            ref[pair_rows(t)] = value
        return carry

    lax.fori_loop(0, target.shape[0] // (2 * slots), sources, 0)


def first_kernel(slots, width, pitch, target, rows, dense, other):
    scatter_rows(slots, 0, width, pitch, target, rows, dense, other)
    dense[...] += other[...]


def last_kernel(slots, first, width, target, rows, before, count, dense, message, other):
    scatter_rows(slots, first, width, width, target, rows, dense, other)
    dense[...] += other[...] + before[...]
    values = dense[0 : dense.shape[0] - 8]
    square = jnp.sum(jnp.sum(values * values, axis=0, keepdims=True), axis=1, keepdims=True)
    touched = jnp.sum(count[...], axis=1, keepdims=True)
    lane = lax.broadcasted_iota(jnp.int32, (1, 128), 1)
    row = jnp.where(lane == 0, square, jnp.where(lane == 1, touched, 0.0))
    message[...] = jnp.broadcast_to(row, message.shape)


def update_kernel(messages, dense, mask, p_in, m_in, v_in, *rest):
    outs, held, made, sems, done = rest[:3], rest[3:6], rest[6:9], rest[9], rest[10]
    size = p_in.shape[0] // STEPS
    spans = [pl.ds(step * size, size) for step in range(STEPS)]
    loads = []
    for step, at in enumerate(spans):
        for k, source in enumerate((p_in, m_in, v_in)):
            copy = pltpu.make_async_copy(source.at[at], held[k].at[at], sems.at[k, step])
            copy.start()
            loads.append(copy)
    total = jnp.sum(messages[...], axis=0, keepdims=True)
    square, touched = total[0:1, 0:1], total[0:1, 1:2]
    rms = jnp.sqrt(square / touched + 1e-06)
    scale = jnp.minimum(jnp.float32(1.0), 0.5 / rms)
    first, second = 0.1 * scale, 0.01 * scale * scale
    copies = []
    for step, at in enumerate(spans):
        for copy in loads[3 * step : 3 * step + 3]:
            copy.wait()
        grad, live = dense[at], mask[at]
        new_m = held[1][at] * (1.0 - 0.1 * live) + first * grad
        new_v = held[2][at] * (1.0 - 0.01 * live) + second * grad * grad
        root = jnp.sqrt(new_v * (1.0 / (1.0 - 0.99**8))) + 1e-08
        made[0][at] = held[0][at] - (live * (0.01 / (1.0 - 0.9**8))) * new_m / root
        made[1][at] = new_m
        made[2][at] = new_v
        for k in range(3):
            copy = pltpu.make_async_copy(made[k].at[at], outs[k].at[at], done.at[k, step])
            copy.start()
            copies.append(copy)
    for copy in copies:
        copy.wait()


def in_hbm(array):
    return pltpu.with_memory_space_constraint(array, pltpu.HBM)


def shape(*dims):
    return jax.ShapeDtypeStruct(dims, f32)


def step(grad_parts, block_ids, block_counts, params, first_moment, second_moment):
    member = lax.axis_index("grp")
    _, _, groups, owners, slots, features, lanes = grad_parts.shape
    blocks = params.shape[0] * params.shape[1]
    devices = groups * owners
    half = owners // 2
    partial = in_hbm(grad_parts.reshape(groups, owners, slots * features, lanes))

    ids = lax.dynamic_index_in_dim(block_ids[0], member, 0, keepdims=False)
    counts = lax.dynamic_index_in_dim(block_counts[0], member, 0, keepdims=False)
    valid = jnp.arange(slots, dtype=jnp.int32)[None, :] < counts[:, None]
    named = jnp.where(valid, ids, blocks).astype(f32)
    named = jnp.pad(named, ((0, 0), (0, lanes - slots)))

    flip, mirror = member ^ 1, 3 - member
    order = jnp.stack([flip, mirror, mirror ^ 1, member])
    flips = [(k, k ^ 1) for k in range(groups)]
    mirrors = [(k, 3 - k) for k in range(groups)]

    def copied(outs, plan):
        return kernel_call(
            functools.partial(copies_kernel, plan),
            outs,
            [SMEM, ANY],
            (VMEM,) * len(outs),
            [pltpu.SemaphoreType.DMA((len(plan),))],
            moved=2 * len(plan) << 18,
        )(order, partial)

    spans = [(sum(CHUNKS[:k]) * features, sum(CHUNKS[: k + 1]) * features) for k in (0, 1)]

    def call(body, outs, ins, single=False):
        specs = VMEM if single else (VMEM,) * len(outs)
        return kernel_call(body, outs, [VMEM] * len(ins), specs)(*ins)

    def permuted(top, low, top_pairs, low_pairs):
        return lax.ppermute(top, "grp", top_pairs), lax.ppermute(low, "grp", low_pairs)

    def exchange(share):
        return lax.all_to_all(share, OWN, split_axis=0, concat_axis=0, tiled=True)

    staged = ((1, 0), (0, 1), (3, 0), (3, 1))

    span = spans[0]
    size = span[1] - span[0]
    piece, both = shape(half, size, lanes), shape(2, half, size, lanes)
    plan = ((0, 0, 0, 0, span), (1, 0, 1, 1, span), (0, 1, 2, 0, span), (1, 1, 2, 1, span))
    top, low = copied((both, both), plan)
    near = permuted(top, low, flips, mirrors)
    plan = tuple((n, None, which, part, span) for n, (which, part) in enumerate(staged))
    kept = copied((piece,) * 4, plan)
    ins = (kept[0], kept[1], *near)
    top, low = call(first_add_kernel, (piece, piece), ins)
    far = permuted(top, low, mirrors, flips)
    pitch = size + 2
    ins = (kept[2], kept[3], *near, *far, named)
    share = call(first_sum_kernel, shape(owners * pitch, lanes), ins, True)
    share = exchange(share.reshape(owners, 1, pitch * lanes))
    named = share[:, 0, size * lanes : size * lanes + slots]
    target = named.astype(jnp.int32).reshape(-1)
    shares = [share.reshape(owners * pitch, lanes)]

    span = spans[1]
    size = span[1] - span[0]
    piece = shape(half, size, lanes)
    plan = ((0, None, 2, 0, span), (1, None, 2, 1, span), (2, None, 0, 0, span), (3, None, 1, 1, span))
    sent = copied((piece,) * 4, plan)
    late = permuted(sent[0], sent[1], flips, mirrors)
    near = permuted(sent[2], sent[3], flips, mirrors)
    plan = tuple((n, None, which, part, span) for n, (which, part) in enumerate(staged))
    kept = copied((piece,) * 4, plan)
    ins = (kept[0], kept[1], *late)
    top, low = call(add_kernel, (piece, piece), ins)
    far = permuted(top, low, mirrors, flips)
    ins = (kept[2], kept[3], *near, *far)
    share = call(sum_kernel, shape(owners, size, lanes), ins, True)
    share = exchange(share)
    shares.append(share.reshape(owners * size, lanes))

    rows = blocks * features
    table = shape(rows + 8, lanes)
    mask, count = kernel_call(
        functools.partial(mark_kernel, slots), (table, shape(1, lanes)), [SMEM], (VMEM, VMEM)
    )(target)
    spare = [pltpu.VMEM(table.shape, f32)]
    before = kernel_call(
        functools.partial(first_kernel, slots, CHUNKS[0], pitch // features), table, [SMEM, VMEM], VMEM, spare
    )(target, shares[0])
    dense, message = kernel_call(
        functools.partial(last_kernel, slots, CHUNKS[0], CHUNKS[1]),
        (table, shape(devices, lanes)),
        [SMEM] + [VMEM] * 3,
        (VMEM, VMEM),
        spare,
    )(target, shares[1], before, count)
    messages = lax.all_to_all(
        message.reshape(devices, 1, lanes), GRP_OWN, split_axis=0, concat_axis=0, tiled=True
    ).reshape(devices, lanes)
    flat = shape(rows, lanes)
    state = [in_hbm(a.reshape(rows, lanes)) for a in (params, first_moment, second_moment)]
    outs = kernel_call(
        update_kernel,
        (flat,) * 3,
        [VMEM] * 3 + [ANY] * 3,
        (ANY,) * 3,
        [pltpu.VMEM((rows, lanes), f32)] * 6 + [pltpu.SemaphoreType.DMA((3, STEPS))] * 2,
    )(messages, dense, mask, *state)
    return tuple(out.reshape(params.shape) for out in outs)


def solution(mesh):
    split = Mesh(
        mesh.devices.reshape(mesh.shape["grp"], 4, 8, 2), ("grp", "own_0", "own_1", "own_2")
    )
    in_specs = (
        P("grp", OWN, None, None, None, None, None),
        P(OWN, None, None, None),
        P(OWN, None, None),
        P(None, GRP_OWN, None, None),
        P(None, GRP_OWN, None, None),
        P(None, GRP_OWN, None, None),
    )
    out_specs = (
        P(None, GRP_OWN, None, None),
        P(None, GRP_OWN, None, None),
        P(None, GRP_OWN, None, None),
    )
    return jax.shard_map(step, mesh=split, in_specs=in_specs, out_specs=out_specs, check_vma=False)
```

```python
import functools

import jax
import jax.numpy as jnp
from jax import lax
from jax.experimental import pallas as pl
from jax.experimental.pallas import tpu as pltpu
from jax.sharding import Mesh
from jax.sharding import PartitionSpec as P


OWN = ("own_0", "own_1", "own_2")
GRP_OWN = ("grp", "own_0", "own_1", "own_2")
CHUNKS = (4, 12)
STEPS = 4
f32 = jnp.float32
ANY = pl.BlockSpec(memory_space=pl.ANY)
VMEM = pl.BlockSpec(memory_space=pltpu.VMEM)
SMEM = pl.BlockSpec(memory_space=pltpu.SMEM)


def kernel_call(body, outs, ins, out_specs, scratch=(), aliases=None, moved=1 << 20):
    return pl.pallas_call(
        body,
        out_shape=outs,
        in_specs=ins,
        out_specs=out_specs,
        scratch_shapes=list(scratch),
        input_output_aliases=aliases or {},
        compiler_params=pltpu.CompilerParams(vmem_limit_bytes=16 << 20),
        cost_estimate=pl.CostEstimate(flops=1 << 18, bytes_accessed=moved, transcendentals=0),
    )


def copies_kernel(plan, order, partial, *rest):
    outs, sems = rest[:-1], rest[-1]
    started = []
    for number, (output, entry, which, part, rows) in enumerate(plan):
        half = partial.shape[1] // 2
        source = partial.at[
            order[which], pl.ds(part * half, half), pl.ds(rows[0], rows[1] - rows[0])
        ]
        target = outs[output] if entry is None else outs[output].at[entry]
        copy = pltpu.make_async_copy(source, target, sems.at[number])
        copy.start()
        started.append(copy)
    for copy in started:
        copy.wait()


def add_kernel(top_own, low_own, top_in, low_in, top_out, low_out):
    top_out[...] = top_own[...] + top_in[...]
    low_out[...] = low_own[...] + low_in[...]


def sum_kernel(top_own, low_own, top_near, low_near, top_far, low_far, out):
    half = top_far.shape[0]
    out[0:half] = top_own[...] + top_near[...] + top_far[...]
    out[half:] = low_own[...] + low_near[...] + low_far[...]


def first_add_kernel(top_own, low_own, top_in, low_in, top_out, low_out):
    top_out[...] = top_own[...] + top_in[1]
    low_out[...] = low_own[...] + low_in[1]


def first_sum_kernel(top_own, low_own, top_near, low_near, top_far, low_far, named, out):
    half, size = top_far.shape[:2]
    pitch = out.shape[0] // (2 * half)
    out[...] = jnp.zeros_like(out)
    for o in range(half):
        out[o * pitch : o * pitch + size] = top_own[o] + top_near[0, o] + top_far[o]
        at = (half + o) * pitch
        out[at : at + size] = low_own[o] + low_near[0, o] + low_far[o]
    for o in range(2 * half):
        at = o * pitch + size
        out[at : at + 1] = named[o : o + 1]


def pair_rows(t):
    return pl.ds(pl.multiple_of(t * 2, 2), 2)


def mark_kernel(slots, target, mask, count):
    mask[...] = jnp.zeros_like(mask)
    ones = jnp.ones((2, mask.shape[1]), f32)

    def source(s, carry):
        for j in range(slots):
            mask[pair_rows(target[s * slots + j])] = ones
        return carry

    lax.fori_loop(0, target.shape[0] // slots, source, 0)
    count[...] = jnp.sum(mask[0 : mask.shape[0] - 8], axis=0, keepdims=True)


def scatter_rows(slots, first, width, pitch, target, rows, even, odd):
    even[...] = jnp.zeros_like(even)
    odd[...] = jnp.zeros_like(odd)

    def sources(s, carry):
        picks = []
        for k, ref in ((0, even), (1, odd)):
            for j in range(width):
                t = target[(2 * s + k) * slots + first + j]
                picks.append((ref, t, (2 * s + k) * pitch + j))
        new = [ref[pair_rows(t)] + rows[pair_rows(at)] for ref, t, at in picks]
        for (ref, t, _), value in zip(picks, new):
            ref[pair_rows(t)] = value
        return carry

    lax.fori_loop(0, target.shape[0] // (2 * slots), sources, 0)


def first_kernel(slots, width, pitch, target, rows, dense, other):
    scatter_rows(slots, 0, width, pitch, target, rows, dense, other)
    dense[...] += other[...]


def last_kernel(slots, first, width, target, rows, before, count, dense, message, other):
    scatter_rows(slots, first, width, width, target, rows, dense, other)
    dense[...] += other[...] + before[...]
    values = dense[0 : dense.shape[0] - 8]
    square = jnp.sum(jnp.sum(values * values, axis=0, keepdims=True), axis=1, keepdims=True)
    touched = jnp.sum(count[...], axis=1, keepdims=True)
    lane = lax.broadcasted_iota(jnp.int32, (1, 128), 1)
    row = jnp.where(lane == 0, square, jnp.where(lane == 1, touched, 0.0))
    message[...] = jnp.broadcast_to(row, message.shape)


def update_kernel(messages, dense, mask, p_in, m_in, v_in, *rest):
    outs, held, made, sems, done = rest[:3], rest[3:6], rest[6:9], rest[9], rest[10]
    size = p_in.shape[0] // STEPS
    spans = [pl.ds(step * size, size) for step in range(STEPS)]
    loads = []
    for step, at in enumerate(spans):
        for k, source in enumerate((p_in, m_in, v_in)):
            copy = pltpu.make_async_copy(source.at[at], held[k].at[at], sems.at[k, step])
            copy.start()
            loads.append(copy)
    total = jnp.sum(messages[...], axis=0, keepdims=True)
    square, touched = total[0:1, 0:1], total[0:1, 1:2]
    rms = jnp.sqrt(square / touched + 1e-06)
    scale = jnp.minimum(jnp.float32(1.0), 0.5 / rms)
    first, second = 0.1 * scale, 0.01 * scale * scale
    copies = []
    for step, at in enumerate(spans):
        for copy in loads[3 * step : 3 * step + 3]:
            copy.wait()
        grad, live = dense[at], mask[at]
        new_m = held[1][at] * (1.0 - 0.1 * live) + first * grad
        new_v = held[2][at] * (1.0 - 0.01 * live) + second * grad * grad
        root = jnp.sqrt(new_v * (1.0 / (1.0 - 0.99**8))) + 1e-08
        made[0][at] = held[0][at] - (live * (0.01 / (1.0 - 0.9**8))) * new_m / root
        made[1][at] = new_m
        made[2][at] = new_v
        for k in range(3):
            copy = pltpu.make_async_copy(made[k].at[at], outs[k].at[at], done.at[k, step])
            copy.start()
            copies.append(copy)
    for copy in copies:
        copy.wait()


def in_hbm(array):
    return pltpu.with_memory_space_constraint(array, pltpu.HBM)


def shape(*dims):
    return jax.ShapeDtypeStruct(dims, f32)


def step(grad_parts, block_ids, block_counts, params, first_moment, second_moment):
    member = lax.axis_index("grp")
    _, _, groups, owners, slots, features, lanes = grad_parts.shape
    blocks = params.shape[0] * params.shape[1]
    devices = groups * owners
    half = owners // 2
    partial = in_hbm(grad_parts.reshape(groups, owners, slots * features, lanes))

    ids = lax.dynamic_index_in_dim(block_ids[0], member, 0, keepdims=False)
    counts = lax.dynamic_index_in_dim(block_counts[0], member, 0, keepdims=False)
    valid = jnp.arange(slots, dtype=jnp.int32)[None, :] < counts[:, None]
    named = jnp.where(valid, ids, blocks).astype(f32)
    named = jnp.pad(named, ((0, 0), (0, lanes - slots)))

    flip, mirror = member ^ 1, 3 - member
    order = jnp.stack([flip, mirror, mirror ^ 1, member])
    flips = [(k, k ^ 1) for k in range(groups)]
    mirrors = [(k, 3 - k) for k in range(groups)]

    def copied(outs, plan):
        return kernel_call(
            functools.partial(copies_kernel, plan),
            outs,
            [SMEM, ANY],
            (VMEM,) * len(outs),
            [pltpu.SemaphoreType.DMA((len(plan),))],
            moved=2 * len(plan) << 18,
        )(order, partial)

    spans = [(sum(CHUNKS[:k]) * features, sum(CHUNKS[: k + 1]) * features) for k in (0, 1)]

    def call(body, outs, ins, single=False):
        specs = VMEM if single else (VMEM,) * len(outs)
        return kernel_call(body, outs, [VMEM] * len(ins), specs)(*ins)

    def permuted(top, low, top_pairs, low_pairs):
        return lax.ppermute(top, "grp", top_pairs), lax.ppermute(low, "grp", low_pairs)

    def exchange(share):
        return lax.all_to_all(share, OWN, split_axis=0, concat_axis=0, tiled=True)

    staged = ((1, 0), (0, 1), (3, 0), (3, 1))

    span = spans[0]
    size = span[1] - span[0]
    piece, both = shape(half, size, lanes), shape(2, half, size, lanes)
    plan = ((0, 0, 0, 0, span), (1, 0, 1, 1, span), (0, 1, 2, 0, span), (1, 1, 2, 1, span))
    top, low = copied((both, both), plan)
    near = permuted(top, low, flips, mirrors)
    plan = tuple((n, None, which, part, span) for n, (which, part) in enumerate(staged))
    kept = copied((piece,) * 4, plan)
    ins = (kept[0], kept[1], *near)
    top, low = call(first_add_kernel, (piece, piece), ins)
    far = permuted(top, low, mirrors, flips)
    pitch = size + 2
    ins = (kept[2], kept[3], *near, *far, named)
    share = call(first_sum_kernel, shape(owners * pitch, lanes), ins, True)
    share = exchange(share.reshape(owners, 1, pitch * lanes))
    named = share[:, 0, size * lanes : size * lanes + slots]
    target = named.astype(jnp.int32).reshape(-1)
    shares = [share.reshape(owners * pitch, lanes)]

    span = spans[1]
    size = span[1] - span[0]
    piece = shape(half, size, lanes)
    sent = copied((piece,) * 2, ((0, None, 2, 0, span), (1, None, 2, 1, span)))
    late = permuted(*sent, flips, mirrors)
    sent = copied((piece,) * 2, ((0, None, 0, 0, span), (1, None, 1, 1, span)))
    near = permuted(*sent, flips, mirrors)
    plan = tuple((n, None, which, part, span) for n, (which, part) in enumerate(staged))
    kept = copied((piece,) * 4, plan)
    ins = (kept[0], kept[1], *late)
    top, low = call(add_kernel, (piece, piece), ins)
    far = permuted(top, low, mirrors, flips)
    ins = (kept[2], kept[3], *near, *far)
    share = call(sum_kernel, shape(owners, size, lanes), ins, True)
    share = exchange(share)
    shares.append(share.reshape(owners * size, lanes))

    rows = blocks * features
    table = shape(rows + 8, lanes)
    mask, count = kernel_call(
        functools.partial(mark_kernel, slots), (table, shape(1, lanes)), [SMEM], (VMEM, VMEM)
    )(target)
    spare = [pltpu.VMEM(table.shape, f32)]
    before = kernel_call(
        functools.partial(first_kernel, slots, CHUNKS[0], pitch // features), table, [SMEM, VMEM], VMEM, spare
    )(target, shares[0])
    dense, message = kernel_call(
        functools.partial(last_kernel, slots, CHUNKS[0], CHUNKS[1]),
        (table, shape(devices, lanes)),
        [SMEM] + [VMEM] * 3,
        (VMEM, VMEM),
        spare,
    )(target, shares[1], before, count)
    messages = lax.all_to_all(
        message.reshape(devices, 1, lanes), GRP_OWN, split_axis=0, concat_axis=0, tiled=True
    ).reshape(devices, lanes)
    flat = shape(rows, lanes)
    state = [in_hbm(a.reshape(rows, lanes)) for a in (params, first_moment, second_moment)]
    outs = kernel_call(
        update_kernel,
        (flat,) * 3,
        [VMEM] * 3 + [ANY] * 3,
        (ANY,) * 3,
        [pltpu.VMEM((rows, lanes), f32)] * 6 + [pltpu.SemaphoreType.DMA((3, STEPS))] * 2,
    )(messages, dense, mask, *state)
    return tuple(out.reshape(params.shape) for out in outs)


def solution(mesh):
    split = Mesh(
        mesh.devices.reshape(mesh.shape["grp"], 4, 8, 2), ("grp", "own_0", "own_1", "own_2")
    )
    in_specs = (
        P("grp", OWN, None, None, None, None, None),
        P(OWN, None, None, None),
        P(OWN, None, None),
        P(None, GRP_OWN, None, None),
        P(None, GRP_OWN, None, None),
        P(None, GRP_OWN, None, None),
    )
    out_specs = (
        P(None, GRP_OWN, None, None),
        P(None, GRP_OWN, None, None),
        P(None, GRP_OWN, None, None),
    )
    return jax.shard_map(step, mesh=split, in_specs=in_specs, out_specs=out_specs, check_vma=False)
```

```python
import functools

import jax
import jax.numpy as jnp
from jax import lax
from jax.experimental import pallas as pl
from jax.experimental.pallas import tpu as pltpu
from jax.sharding import Mesh
from jax.sharding import PartitionSpec as P


OWN = ("own_0", "own_1", "own_2")
GRP_OWN = ("grp", "own_0", "own_1", "own_2")
CHUNKS = (4, 12)
STEPS = 4
f32 = jnp.float32
ANY = pl.BlockSpec(memory_space=pl.ANY)
VMEM = pl.BlockSpec(memory_space=pltpu.VMEM)
SMEM = pl.BlockSpec(memory_space=pltpu.SMEM)


def kernel_call(body, outs, ins, out_specs, scratch=(), aliases=None, moved=1 << 20):
    return pl.pallas_call(
        body,
        out_shape=outs,
        in_specs=ins,
        out_specs=out_specs,
        scratch_shapes=list(scratch),
        input_output_aliases=aliases or {},
        compiler_params=pltpu.CompilerParams(vmem_limit_bytes=16 << 20),
        cost_estimate=pl.CostEstimate(flops=1 << 18, bytes_accessed=moved, transcendentals=0),
    )


def copies_kernel(plan, order, partial, *rest):
    outs, sems = rest[:-1], rest[-1]
    started = []
    for number, (output, entry, which, part, rows) in enumerate(plan):
        half = partial.shape[1] // 2
        source = partial.at[
            order[which], pl.ds(part * half, half), pl.ds(rows[0], rows[1] - rows[0])
        ]
        target = outs[output] if entry is None else outs[output].at[entry]
        copy = pltpu.make_async_copy(source, target, sems.at[number])
        copy.start()
        started.append(copy)
    for copy in started:
        copy.wait()


def add_kernel(top_own, low_own, top_in, low_in, top_out, low_out):
    top_out[...] = top_own[...] + top_in[...]
    low_out[...] = low_own[...] + low_in[...]


def first_add_kernel(top_own, low_own, top_in, low_in, top_out, low_out):
    top_out[...] = top_own[...] + top_in[1]
    low_out[...] = low_own[...] + low_in[1]


def first_sum_kernel(top_own, low_own, top_near, low_near, top_far, low_far, out):
    half = top_far.shape[0]
    out[0:half] = top_own[...] + top_near[0] + top_far[...]
    out[half:] = low_own[...] + low_near[0] + low_far[...]


def join_kernel(top_own, low_own, top_near, low_near, top_far, low_far, before, out):
    half, done = top_far.shape[0], before.shape[1]
    out[:, 0:done] = before[...]
    out[0:half, done:] = top_own[...] + top_near[...] + top_far[...]
    out[half:, done:] = low_own[...] + low_near[...] + low_far[...]


def pair_rows(t):
    return pl.ds(pl.multiple_of(t * 2, 2), 2)


def mark_kernel(slots, target, mask, count):
    mask[...] = jnp.zeros_like(mask)
    ones = jnp.ones((2, mask.shape[1]), f32)

    def source(s, carry):
        for j in range(slots):
            mask[pair_rows(target[s * slots + j])] = ones
        return carry

    lax.fori_loop(0, target.shape[0] // slots, source, 0)
    count[...] = jnp.sum(mask[0 : mask.shape[0] - 8], axis=0, keepdims=True)


def scatter_rows(slots, first, width, pitch, target, rows, even, odd):
    even[...] = jnp.zeros_like(even)
    odd[...] = jnp.zeros_like(odd)

    def sources(s, carry):
        picks = []
        for k, ref in ((0, even), (1, odd)):
            for j in range(width):
                t = target[(2 * s + k) * slots + first + j]
                picks.append((ref, t, (2 * s + k) * pitch + j))
        new = [ref[pair_rows(t)] + rows[pair_rows(at)] for ref, t, at in picks]
        for (ref, t, _), value in zip(picks, new):
            ref[pair_rows(t)] = value
        return carry

    lax.fori_loop(0, target.shape[0] // (2 * slots), sources, 0)


def scatter_kernel(slots, target, rows, count, dense, message, other):
    scatter_rows(slots, 0, slots, slots, target, rows, dense, other)
    dense[...] += other[...]
    values = dense[0 : dense.shape[0] - 8]
    square = jnp.sum(jnp.sum(values * values, axis=0, keepdims=True), axis=1, keepdims=True)
    touched = jnp.sum(count[...], axis=1, keepdims=True)
    lane = lax.broadcasted_iota(jnp.int32, (1, 128), 1)
    row = jnp.where(lane == 0, square, jnp.where(lane == 1, touched, 0.0))
    message[...] = jnp.broadcast_to(row, message.shape)


def update_kernel(messages, dense, mask, p_in, m_in, v_in, *rest):
    outs, held, made, sems, done = rest[:3], rest[3:6], rest[6:9], rest[9], rest[10]
    size = p_in.shape[0] // STEPS
    spans = [pl.ds(step * size, size) for step in range(STEPS)]
    loads = []
    for step, at in enumerate(spans):
        for k, source in enumerate((p_in, m_in, v_in)):
            copy = pltpu.make_async_copy(source.at[at], held[k].at[at], sems.at[k, step])
            copy.start()
            loads.append(copy)
    total = jnp.sum(messages[...], axis=0, keepdims=True)
    square, touched = total[0:1, 0:1], total[0:1, 1:2]
    rms = jnp.sqrt(square / touched + 1e-06)
    scale = jnp.minimum(jnp.float32(1.0), 0.5 / rms)
    first, second = 0.1 * scale, 0.01 * scale * scale
    copies = []
    for step, at in enumerate(spans):
        for copy in loads[3 * step : 3 * step + 3]:
            copy.wait()
        grad, live = dense[at], mask[at]
        new_m = held[1][at] * (1.0 - 0.1 * live) + first * grad
        new_v = held[2][at] * (1.0 - 0.01 * live) + second * grad * grad
        root = jnp.sqrt(new_v * (1.0 / (1.0 - 0.99**8))) + 1e-08
        made[0][at] = held[0][at] - (live * (0.01 / (1.0 - 0.9**8))) * new_m / root
        made[1][at] = new_m
        made[2][at] = new_v
        for k in range(3):
            copy = pltpu.make_async_copy(made[k].at[at], outs[k].at[at], done.at[k, step])
            copy.start()
            copies.append(copy)
    for copy in copies:
        copy.wait()


def in_hbm(array):
    return pltpu.with_memory_space_constraint(array, pltpu.HBM)


def shape(*dims):
    return jax.ShapeDtypeStruct(dims, f32)


def step(grad_parts, block_ids, block_counts, params, first_moment, second_moment):
    member = lax.axis_index("grp")
    _, _, groups, owners, slots, features, lanes = grad_parts.shape
    blocks = params.shape[0] * params.shape[1]
    devices = groups * owners
    half = owners // 2
    partial = in_hbm(grad_parts.reshape(groups, owners, slots * features, lanes))

    ids = lax.dynamic_index_in_dim(block_ids[0], member, 0, keepdims=False)
    counts = lax.dynamic_index_in_dim(block_counts[0], member, 0, keepdims=False)
    valid = jnp.arange(slots, dtype=jnp.int32)[None, :] < counts[:, None]
    named = jnp.where(valid, ids, blocks).astype(f32)
    named = jnp.pad(named, ((0, 0), (0, lanes - slots))).reshape(owners, 1, lanes)
    named = lax.all_to_all(named, OWN, split_axis=0, concat_axis=0, tiled=True)
    target = named.reshape(owners, lanes)[:, :slots].astype(jnp.int32).reshape(-1)

    flip, mirror = member ^ 1, 3 - member
    order = jnp.stack([flip, mirror, mirror ^ 1, member])
    flips = [(k, k ^ 1) for k in range(groups)]
    mirrors = [(k, 3 - k) for k in range(groups)]

    def copied(outs, plan):
        return kernel_call(
            functools.partial(copies_kernel, plan),
            outs,
            [SMEM, ANY],
            (VMEM,) * len(outs),
            [pltpu.SemaphoreType.DMA((len(plan),))],
            moved=2 * len(plan) << 18,
        )(order, partial)

    spans = [(sum(CHUNKS[:k]) * features, sum(CHUNKS[: k + 1]) * features) for k in (0, 1)]

    def call(body, outs, ins, single=False):
        specs = VMEM if single else (VMEM,) * len(outs)
        return kernel_call(body, outs, [VMEM] * len(ins), specs)(*ins)

    def permuted(top, low, top_pairs, low_pairs):
        return lax.ppermute(top, "grp", top_pairs), lax.ppermute(low, "grp", low_pairs)

    staged = ((1, 0), (0, 1), (3, 0), (3, 1))

    span = spans[0]
    size = span[1] - span[0]
    piece, both = shape(half, size, lanes), shape(2, half, size, lanes)
    plan = ((0, 0, 0, 0, span), (1, 0, 1, 1, span), (0, 1, 2, 0, span), (1, 1, 2, 1, span))
    top, low = copied((both, both), plan)
    near = permuted(top, low, flips, mirrors)
    plan = tuple((n, None, which, part, span) for n, (which, part) in enumerate(staged))
    kept = copied((piece,) * 4, plan)
    ins = (kept[0], kept[1], *near)
    top, low = call(first_add_kernel, (piece, piece), ins)
    far = permuted(top, low, mirrors, flips)
    ins = (kept[2], kept[3], *near, *far)
    before = call(first_sum_kernel, shape(owners, size, lanes), ins, True)

    span = spans[1]
    size = span[1] - span[0]
    piece = shape(half, size, lanes)
    sent = copied((piece,) * 2, ((0, None, 2, 0, span), (1, None, 2, 1, span)))
    late = permuted(*sent, flips, mirrors)
    sent = copied((piece,) * 2, ((0, None, 0, 0, span), (1, None, 1, 1, span)))
    near = permuted(*sent, flips, mirrors)
    plan = tuple((n, None, which, part, span) for n, (which, part) in enumerate(staged))
    kept = copied((piece,) * 4, plan)
    ins = (kept[0], kept[1], *late)
    top, low = call(add_kernel, (piece, piece), ins)
    far = permuted(top, low, mirrors, flips)
    ins = (kept[2], kept[3], *near, *far, before)
    share = call(join_kernel, shape(owners, span[1], lanes), ins, True)
    share = lax.all_to_all(share, OWN, split_axis=0, concat_axis=0, tiled=True)
    share = share.reshape(owners * slots * features, lanes)

    rows = blocks * features
    table = shape(rows + 8, lanes)
    mask, count = kernel_call(
        functools.partial(mark_kernel, slots), (table, shape(1, lanes)), [SMEM], (VMEM, VMEM)
    )(target)
    dense, message = kernel_call(
        functools.partial(scatter_kernel, slots),
        (table, shape(devices, lanes)),
        [SMEM, VMEM, VMEM],
        (VMEM, VMEM),
        [pltpu.VMEM(table.shape, f32)],
    )(target, share, count)
    messages = lax.all_to_all(
        message.reshape(devices, 1, lanes), GRP_OWN, split_axis=0, concat_axis=0, tiled=True
    ).reshape(devices, lanes)
    flat = shape(rows, lanes)
    state = [in_hbm(a.reshape(rows, lanes)) for a in (params, first_moment, second_moment)]
    outs = kernel_call(
        update_kernel,
        (flat,) * 3,
        [VMEM] * 3 + [ANY] * 3,
        (ANY,) * 3,
        [pltpu.VMEM((rows, lanes), f32)] * 6 + [pltpu.SemaphoreType.DMA((3, STEPS))] * 2,
    )(messages, dense, mask, *state)
    return tuple(out.reshape(params.shape) for out in outs)


def solution(mesh):
    split = Mesh(
        mesh.devices.reshape(mesh.shape["grp"], 4, 8, 2), ("grp", "own_0", "own_1", "own_2")
    )
    in_specs = (
        P("grp", OWN, None, None, None, None, None),
        P(OWN, None, None, None),
        P(OWN, None, None),
        P(None, GRP_OWN, None, None),
        P(None, GRP_OWN, None, None),
        P(None, GRP_OWN, None, None),
    )
    out_specs = (
        P(None, GRP_OWN, None, None),
        P(None, GRP_OWN, None, None),
        P(None, GRP_OWN, None, None),
    )
    return jax.shard_map(step, mesh=split, in_specs=in_specs, out_specs=out_specs, check_vma=False)
```

```python
import functools

import jax
import jax.numpy as jnp
from jax import lax
from jax.experimental import pallas as pl
from jax.experimental.pallas import tpu as pltpu
from jax.sharding import Mesh
from jax.sharding import PartitionSpec as P


OWN = ("own_0", "own_1", "own_2")
GRP_OWN = ("grp", "own_0", "own_1", "own_2")
CHUNKS = (4, 12)
STEPS = 8
f32 = jnp.float32
ANY = pl.BlockSpec(memory_space=pl.ANY)
VMEM = pl.BlockSpec(memory_space=pltpu.VMEM)
SMEM = pl.BlockSpec(memory_space=pltpu.SMEM)


def kernel_call(body, outs, ins, out_specs, scratch=(), aliases=None, moved=1 << 20):
    return pl.pallas_call(
        body,
        out_shape=outs,
        in_specs=ins,
        out_specs=out_specs,
        scratch_shapes=list(scratch),
        input_output_aliases=aliases or {},
        compiler_params=pltpu.CompilerParams(vmem_limit_bytes=16 << 20),
        cost_estimate=pl.CostEstimate(flops=1 << 18, bytes_accessed=moved, transcendentals=0),
    )


def copies_kernel(plan, order, partial, *rest):
    outs, sems = rest[:-1], rest[-1]
    started = []
    for number, (output, entry, which, part, rows) in enumerate(plan):
        half = partial.shape[1] // 2
        source = partial.at[
            order[which], pl.ds(part * half, half), pl.ds(rows[0], rows[1] - rows[0])
        ]
        target = outs[output] if entry is None else outs[output].at[entry]
        copy = pltpu.make_async_copy(source, target, sems.at[number])
        copy.start()
        started.append(copy)
    for copy in started:
        copy.wait()


def add_kernel(top_own, low_own, top_in, low_in, top_out, low_out):
    top_out[...] = top_own[...] + top_in[...]
    low_out[...] = low_own[...] + low_in[...]


def sum_kernel(top_own, low_own, top_near, low_near, top_far, low_far, out):
    half = top_far.shape[0]
    out[0:half] = top_own[...] + top_near[...] + top_far[...]
    out[half:] = low_own[...] + low_near[...] + low_far[...]


def first_add_kernel(top_own, low_own, top_in, low_in, top_out, low_out):
    top_out[...] = top_own[...] + top_in[1]
    low_out[...] = low_own[...] + low_in[1]


def first_sum_kernel(top_own, low_own, top_near, low_near, top_far, low_far, named, out):
    half, size = top_far.shape[:2]
    pitch = out.shape[0] // (2 * half)
    out[...] = jnp.zeros_like(out)
    for o in range(half):
        out[o * pitch : o * pitch + size] = top_own[o] + top_near[0, o] + top_far[o]
        at = (half + o) * pitch
        out[at : at + size] = low_own[o] + low_near[0, o] + low_far[o]
    for o in range(2 * half):
        at = o * pitch + size
        out[at : at + 1] = named[o : o + 1]


def pair_rows(t):
    return pl.ds(pl.multiple_of(t * 2, 2), 2)


def mark_kernel(slots, target, mask, count):
    mask[...] = jnp.zeros_like(mask)
    ones = jnp.ones((2, mask.shape[1]), f32)

    def source(s, carry):
        for j in range(slots):
            mask[pair_rows(target[s * slots + j])] = ones
        return carry

    lax.fori_loop(0, target.shape[0] // slots, source, 0)
    count[...] = jnp.sum(mask[0 : mask.shape[0] - 8], axis=0, keepdims=True)


def scatter_rows(slots, first, width, pitch, target, rows, even, odd):
    even[...] = jnp.zeros_like(even)
    odd[...] = jnp.zeros_like(odd)

    def sources(s, carry):
        picks = []
        for k, ref in ((0, even), (1, odd)):
            for j in range(width):
                t = target[(2 * s + k) * slots + first + j]
                picks.append((ref, t, (2 * s + k) * pitch + j))
        new = [ref[pair_rows(t)] + rows[pair_rows(at)] for ref, t, at in picks]
        for (ref, t, _), value in zip(picks, new):
            ref[pair_rows(t)] = value
        return carry

    lax.fori_loop(0, target.shape[0] // (2 * slots), sources, 0)


def first_kernel(slots, width, pitch, target, rows, dense, other):
    scatter_rows(slots, 0, width, pitch, target, rows, dense, other)
    dense[...] += other[...]


def last_kernel(slots, first, width, target, rows, before, count, dense, message, other):
    scatter_rows(slots, first, width, width, target, rows, dense, other)
    dense[...] += other[...] + before[...]
    values = dense[0 : dense.shape[0] - 8]
    square = jnp.sum(jnp.sum(values * values, axis=0, keepdims=True), axis=1, keepdims=True)
    touched = jnp.sum(count[...], axis=1, keepdims=True)
    lane = lax.broadcasted_iota(jnp.int32, (1, 128), 1)
    row = jnp.where(lane == 0, square, jnp.where(lane == 1, touched, 0.0))
    message[...] = jnp.broadcast_to(row, message.shape)


def update_kernel(messages, dense, mask, p_in, m_in, v_in, *rest):
    outs, held, made, sems, done = rest[:3], rest[3:6], rest[6:9], rest[9], rest[10]
    size = p_in.shape[0] // STEPS
    spans = [pl.ds(step * size, size) for step in range(STEPS)]
    loads = []
    for step, at in enumerate(spans):
        for k, source in enumerate((p_in, m_in, v_in)):
            copy = pltpu.make_async_copy(source.at[at], held[k].at[at], sems.at[k, step])
            copy.start()
            loads.append(copy)
    total = jnp.sum(messages[...], axis=0, keepdims=True)
    square, touched = total[0:1, 0:1], total[0:1, 1:2]
    rms = jnp.sqrt(square / touched + 1e-06)
    scale = jnp.minimum(jnp.float32(1.0), 0.5 / rms)
    first, second = 0.1 * scale, 0.01 * scale * scale
    copies = []
    for step, at in enumerate(spans):
        for copy in loads[3 * step : 3 * step + 3]:
            copy.wait()
        grad, live = dense[at], mask[at]
        new_m = held[1][at] * (1.0 - 0.1 * live) + first * grad
        new_v = held[2][at] * (1.0 - 0.01 * live) + second * grad * grad
        root = jnp.sqrt(new_v * (1.0 / (1.0 - 0.99**8))) + 1e-08
        made[0][at] = held[0][at] - (live * (0.01 / (1.0 - 0.9**8))) * new_m / root
        made[1][at] = new_m
        made[2][at] = new_v
        for k in range(3):
            copy = pltpu.make_async_copy(made[k].at[at], outs[k].at[at], done.at[k, step])
            copy.start()
            copies.append(copy)
    for copy in copies:
        copy.wait()


def in_hbm(array):
    return pltpu.with_memory_space_constraint(array, pltpu.HBM)


def shape(*dims):
    return jax.ShapeDtypeStruct(dims, f32)


def step(grad_parts, block_ids, block_counts, params, first_moment, second_moment):
    member = lax.axis_index("grp")
    _, _, groups, owners, slots, features, lanes = grad_parts.shape
    blocks = params.shape[0] * params.shape[1]
    devices = groups * owners
    half = owners // 2
    partial = in_hbm(grad_parts.reshape(groups, owners, slots * features, lanes))

    ids = lax.dynamic_index_in_dim(block_ids[0], member, 0, keepdims=False)
    counts = lax.dynamic_index_in_dim(block_counts[0], member, 0, keepdims=False)
    valid = jnp.arange(slots, dtype=jnp.int32)[None, :] < counts[:, None]
    named = jnp.where(valid, ids, blocks).astype(f32)
    named = jnp.pad(named, ((0, 0), (0, lanes - slots)))

    flip, mirror = member ^ 1, 3 - member
    order = jnp.stack([flip, mirror, mirror ^ 1, member])
    flips = [(k, k ^ 1) for k in range(groups)]
    mirrors = [(k, 3 - k) for k in range(groups)]

    def copied(outs, plan):
        return kernel_call(
            functools.partial(copies_kernel, plan),
            outs,
            [SMEM, ANY],
            (VMEM,) * len(outs),
            [pltpu.SemaphoreType.DMA((len(plan),))],
            moved=2 * len(plan) << 18,
        )(order, partial)

    spans = [(sum(CHUNKS[:k]) * features, sum(CHUNKS[: k + 1]) * features) for k in (0, 1)]

    def call(body, outs, ins, single=False):
        specs = VMEM if single else (VMEM,) * len(outs)
        return kernel_call(body, outs, [VMEM] * len(ins), specs)(*ins)

    def permuted(top, low, top_pairs, low_pairs):
        return lax.ppermute(top, "grp", top_pairs), lax.ppermute(low, "grp", low_pairs)

    def exchange(share):
        return lax.all_to_all(share, OWN, split_axis=0, concat_axis=0, tiled=True)

    staged = ((1, 0), (0, 1), (3, 0), (3, 1))

    span = spans[0]
    size = span[1] - span[0]
    piece, both = shape(half, size, lanes), shape(2, half, size, lanes)
    plan = ((0, 0, 0, 0, span), (1, 0, 1, 1, span), (0, 1, 2, 0, span), (1, 1, 2, 1, span))
    top, low = copied((both, both), plan)
    near = permuted(top, low, flips, mirrors)
    plan = tuple((n, None, which, part, span) for n, (which, part) in enumerate(staged))
    kept = copied((piece,) * 4, plan)
    ins = (kept[0], kept[1], *near)
    top, low = call(first_add_kernel, (piece, piece), ins)
    far = permuted(top, low, mirrors, flips)
    pitch = size + 2
    ins = (kept[2], kept[3], *near, *far, named)
    share = call(first_sum_kernel, shape(owners * pitch, lanes), ins, True)
    share = exchange(share.reshape(owners, 1, pitch * lanes))
    named = share[:, 0, size * lanes : size * lanes + slots]
    target = named.astype(jnp.int32).reshape(-1)
    shares = [share.reshape(owners * pitch, lanes)]

    span = spans[1]
    size = span[1] - span[0]
    piece = shape(half, size, lanes)
    sent = copied((piece,) * 2, ((0, None, 2, 0, span), (1, None, 2, 1, span)))
    late = permuted(*sent, flips, mirrors)
    sent = copied((piece,) * 2, ((0, None, 0, 0, span), (1, None, 1, 1, span)))
    near = permuted(*sent, flips, mirrors)
    kept = copied((piece,) * 2, ((0, None, 1, 0, span), (1, None, 0, 1, span)))
    top, low = call(add_kernel, (piece, piece), (*kept, *late))
    far = permuted(top, low, mirrors, flips)
    kept = copied((piece,) * 2, ((0, None, 3, 0, span), (1, None, 3, 1, span)))
    ins = (*kept, *near, *far)
    share = call(sum_kernel, shape(owners, size, lanes), ins, True)
    share = exchange(share)
    shares.append(share.reshape(owners * size, lanes))

    rows = blocks * features
    table = shape(rows + 8, lanes)
    mask, count = kernel_call(
        functools.partial(mark_kernel, slots), (table, shape(1, lanes)), [SMEM], (VMEM, VMEM)
    )(target)
    spare = [pltpu.VMEM(table.shape, f32)]
    before = kernel_call(
        functools.partial(first_kernel, slots, CHUNKS[0], pitch // features), table, [SMEM, VMEM], VMEM, spare
    )(target, shares[0])
    dense, message = kernel_call(
        functools.partial(last_kernel, slots, CHUNKS[0], CHUNKS[1]),
        (table, shape(devices, lanes)),
        [SMEM] + [VMEM] * 3,
        (VMEM, VMEM),
        spare,
    )(target, shares[1], before, count)
    messages = lax.all_to_all(
        message.reshape(devices, 1, lanes), GRP_OWN, split_axis=0, concat_axis=0, tiled=True
    ).reshape(devices, lanes)
    flat = shape(rows, lanes)
    state = [in_hbm(a.reshape(rows, lanes)) for a in (params, first_moment, second_moment)]
    outs = kernel_call(
        update_kernel,
        (flat,) * 3,
        [VMEM] * 3 + [ANY] * 3,
        (ANY,) * 3,
        [pltpu.VMEM((rows, lanes), f32)] * 6 + [pltpu.SemaphoreType.DMA((3, STEPS))] * 2,
    )(messages, dense, mask, *state)
    return tuple(out.reshape(params.shape) for out in outs)


def solution(mesh):
    split = Mesh(
        mesh.devices.reshape(mesh.shape["grp"], 4, 8, 2), ("grp", "own_0", "own_1", "own_2")
    )
    in_specs = (
        P("grp", OWN, None, None, None, None, None),
        P(OWN, None, None, None),
        P(OWN, None, None),
        P(None, GRP_OWN, None, None),
        P(None, GRP_OWN, None, None),
        P(None, GRP_OWN, None, None),
    )
    out_specs = (
        P(None, GRP_OWN, None, None),
        P(None, GRP_OWN, None, None),
        P(None, GRP_OWN, None, None),
    )
    return jax.shard_map(step, mesh=split, in_specs=in_specs, out_specs=out_specs, check_vma=False)
```
